128 devices in a mesh: tile: 32 (over x, z, core), cuts: 4 (over y).
Axes of the slice: x: 4, y: 4, z: 4, core: 2. Of those that a mesh axis runs over, the one named last changes fastest.
Arguments:
- amplitudes: float32 [1024, 128, 128], P(('tile', 'cuts')), may hold values from 0 to 2
- positions: int32 [1024, 2], replicated, may hold values from 0 to 3968, as said below
- probe_field: float32 [2, 128, 128], replicated, may hold values from -4 to 4
- object_slices: float32 [4, 2, 256, 4096], P('cuts', None, None, 'tile'), may hold values from -1 to 1, as said below
Outputs:
- refined_object: float32 [4, 2, 256, 4096], P('cuts', None, None, 'tile')
The draws below stay inside these ranges and needn't reach their ends.
Inputs may be any that keep to these rules, and one draw needn't show every extreme that they name: `positions`: rows lie in 0 .. 128; every frame's 128 columns lie inside the 4096 columns. A frame's owner tile is its column // 128. Frames are read in blocks of 8 consecutive frames, one block per device of tile+cuts in mesh order; one block holds at most 2 frames of any owner tile, and some block holds exactly 2. For every cuts index, the blocks of that index hold at most 16 frames of any one owner tile, and in every draw some owner tile receives exactly 16 from them. `object_slices`: transmissions have modulus at most 1.
All inputs are finite; a program needn't handle non-finite values.
Results may differ from the reference program's by a relative error of at most 0.015.
Values may be sent and summed in bfloat16 or wider, within the bound.
A program may use at most 128 MiB of HBM per device.

```python
import math
import jax
import jax.numpy as jnp
from jax import lax

M = 128
SLICES = 4
ITERS = 2
H = 256
W = 128
FR_DEV = 8
CAP = 2
FRAMES = 1024
N_TILE = 32
N_CUTS = 4


def draw_positions(key, part):
    tile_count = N_TILE
    cut_count = N_CUTS
    frames_held = FR_DEV
    capacity = CAP
    keys_list = jax.random.split(key, 3)
    pattern = jnp.array([2 * frames_held, frames_held, frames_held // 2, frames_held // 2], jnp.int32)
    loads = jnp.tile(pattern, tile_count // 4)
    bounds = jnp.cumsum(loads)
    token = jnp.arange(tile_count * frames_held, dtype=jnp.int32)
    position_index = jnp.sum((token[:, None] >= bounds[None, :]).astype(jnp.int32), axis=1)
    group_index = token // capacity
    dealt = group_index % tile_count
    within = group_index // tile_count * capacity + token % capacity

    def one_cut(sub_key):
        first_key, second_key, third_key = jax.random.split(sub_key, 3)
        tile_order = jax.random.permutation(first_key, tile_count)
        reader_order = jax.random.permutation(second_key, tile_count)
        shuffles = jax.vmap(lambda each_key: jax.random.permutation(each_key, frames_held))(jax.random.split(third_key, tile_count))
        reader_id = reader_order[dealt]
        slot_id = shuffles[reader_id, within]
        return jnp.zeros((tile_count, frames_held), jnp.int32).at[reader_id, slot_id].set(tile_order[position_index].astype(jnp.int32))
    owners = jax.vmap(one_cut)(jax.random.split(keys_list[0], cut_count))
    owners = jnp.transpose(owners, (1, 0, 2)).reshape(tile_count * cut_count * frames_held)
    upper_bound = jnp.where(owners == tile_count - 1, W - M + 1, W)
    across = jax.random.randint(keys_list[1], owners.shape, 0, upper_bound)
    frame_ids = jnp.arange(owners.shape[0], dtype=jnp.int32)
    last_first = jnp.argmax((owners == tile_count - 1).astype(jnp.int32)).astype(jnp.int32)
    zero_first = jnp.argmax((owners == 0).astype(jnp.int32)).astype(jnp.int32)
    across = jnp.where(frame_ids == last_first, W - M, across)
    across = jnp.where(frame_ids == zero_first, 0, across)
    downward = jax.random.randint(keys_list[2], owners.shape, 0, H - M + 1)
    columns = owners * W + across
    return jnp.stack([downward, columns], axis=1).astype(jnp.int32)


def draw_object_slices(key, part):
    first_key, second_key = jax.random.split(key)
    shape = (SLICES, H, W * N_TILE)
    phase = jax.random.uniform(first_key, shape, jnp.float32, -jnp.pi, jnp.pi)
    modulus = jax.random.uniform(second_key, shape, jnp.float32, 0.8, 1.0)
    return jnp.stack([modulus * jnp.cos(phase), modulus * jnp.sin(phase)], axis=1).astype(jnp.float32)


def level_of(stream_key, extent, cuts, least, high):
    factor_of = 1.0
    for axis_at, shards_of in cuts:
        draws = jax.random.uniform(jax.random.fold_in(jax.random.fold_in(stream_key, 6), axis_at), (shards_of,), jnp.float32, least / len(cuts), high / len(cuts))
        factor_of = factor_of * jnp.repeat(jnp.exp(draws), extent[axis_at] // shards_of).reshape((-1,) + (1,) * (len(extent) - 1 - axis_at))
    return factor_of


def normal_values(rng, dims, width, reach, kind=jnp.bfloat16):
    values = width * jax.random.normal(rng, dims, jnp.float32)
    return jnp.clip(values, min=-reach, max=reach).astype(kind)


def setup_inputs(seed: int = 0) -> dict:
    keys = jax.random.split(jax.random.key(seed), 5)
    return {
        "amplitudes": jnp.clip(2.0 * jax.random.uniform(keys[0], (FRAMES, M, M), jnp.float32) ** level_of(keys[0], (FRAMES, M, M), ((0, 128),), -0.2, 0.2), 0.0, 2.0),
        "positions": draw_positions(jax.random.fold_in(keys[4], 71), 0),
        "probe_field": normal_values(keys[2], (2, M, M), 0.7, 4.0, jnp.float32),
        "object_slices": draw_object_slices(jax.random.fold_in(keys[4], 71), 0),
    }


STEP_SIZE = 0.05
AMPLITUDE_FLOOR = 0.25

def block_table(real_part, imag_part):
    upper = jnp.stack([real_part, imag_part], axis=1)
    lower = jnp.stack([-imag_part, real_part], axis=1)
    return jnp.stack([upper, lower], axis=0).astype(jnp.bfloat16)

def make_tables(frame_side):
    highest = lax.Precision.HIGHEST
    index = jnp.arange(frame_side, dtype=jnp.int32)
    product = index[:, None] * index[None, :] % frame_side
    angle = product.astype(jnp.float32) * (2.0 * math.pi / frame_side)
    norm_scale = 1.0 / math.sqrt(frame_side)
    four_real = jnp.cos(angle) * norm_scale
    four_imag = -jnp.sin(angle) * norm_scale
    centred = (index + frame_side // 2) % frame_side - frame_side // 2
    chirp = -math.pi * (centred * centred).astype(jnp.float32) / (4.0 * frame_side)
    chirp_real = jnp.cos(chirp)
    chirp_imag = jnp.sin(chirp)
    left_real = four_real * chirp_real[None, :] + four_imag * chirp_imag[None, :]
    left_imag = four_real * chirp_imag[None, :] - four_imag * chirp_real[None, :]
    prop_real = jnp.dot(left_real, four_real, precision=highest) - jnp.dot(left_imag, four_imag, precision=highest)
    prop_imag = jnp.dot(left_real, four_imag, precision=highest) + jnp.dot(left_imag, four_real, precision=highest)
    return (block_table(four_real, four_imag), block_table(four_real, -four_imag), block_table(prop_real, prop_imag), block_table(prop_real, -prop_imag))

def right_product(field, table):
    rounded = lax.optimization_barrier(field.astype(jnp.bfloat16)).astype(jnp.float32)
    return jnp.einsum('fcij,cjdk->fdik', rounded, table.astype(jnp.float32), precision=lax.Precision.HIGHEST)

def two_sided(field, table):
    first = right_product(field, table)
    second = right_product(jnp.swapaxes(first, -1, -2), table)
    return jnp.swapaxes(second, -1, -2)

def complex_times(left, right):
    real_part = left[..., 0, :, :] * right[..., 0, :, :] - left[..., 1, :, :] * right[..., 1, :, :]
    imag_part = left[..., 0, :, :] * right[..., 1, :, :] + left[..., 1, :, :] * right[..., 0, :, :]
    return jnp.stack([real_part, imag_part], axis=-3)

def conj_times(left, right):
    real_part = left[..., 0, :, :] * right[..., 0, :, :] + left[..., 1, :, :] * right[..., 1, :, :]
    imag_part = left[..., 0, :, :] * right[..., 1, :, :] - left[..., 1, :, :] * right[..., 0, :, :]
    return jnp.stack([real_part, imag_part], axis=-3)

def frame_patches(windows, probe_field, measured, tables):
    four, four_conj, prop, prop_conj = tables
    slice_count = windows.shape[1]
    wave = complex_times(probe_field[None], windows[:, 0].astype(jnp.float32))
    fields = []
    for level in range(1, slice_count):
        moved = two_sided(wave, prop)
        fields.append(moved)
        wave = complex_times(windows[:, level].astype(jnp.float32), moved)
    far = two_sided(wave, four)
    magnitude = jnp.sqrt(far[:, 0] * far[:, 0] + far[:, 1] * far[:, 1])
    factor = 1.0 - measured / jnp.maximum(magnitude, AMPLITUDE_FLOOR)
    back = two_sided(far * factor[:, None], four_conj)
    patches = [None] * slice_count
    for level in range(slice_count - 1, 0, -1):
        patches[level] = conj_times(fields[level - 1], back)
        back = two_sided(conj_times(windows[:, level].astype(jnp.float32), back), prop_conj)
    patches[0] = conj_times(probe_field[None], back)
    return jnp.stack(patches, axis=1)

def cut_windows(panel, frame_rows, frame_cols, frame_side):
    zero_index = jnp.zeros((), jnp.int32)

    def window_at(row_start, col_start):
        start = (zero_index, zero_index, row_start.astype(jnp.int32), col_start.astype(jnp.int32))
        return lax.dynamic_slice(panel, start, (panel.shape[0], panel.shape[1], frame_side, frame_side))
    return jax.vmap(window_at)(frame_rows, frame_cols)

def place_patches(accum, patches, frame_rows, frame_cols, weights):
    zero_index = jnp.zeros((), jnp.int32)

    def add_patch(frame_index, current):
        start = (zero_index, zero_index, frame_rows[frame_index].astype(jnp.int32), frame_cols[frame_index].astype(jnp.int32))
        region = lax.dynamic_slice(current, start, patches.shape[1:])
        return lax.dynamic_update_slice(current, region + patches[frame_index] * weights[frame_index], start)
    return lax.fori_loop(0, patches.shape[0], add_patch, accum)

def reference(amplitudes, positions, probe_field, object_slices):
    tables = make_tables(M)
    current = object_slices
    block_count = positions.shape[0] // FR_DEV
    weights = jnp.ones((FR_DEV,), jnp.float32)
    for turn in range(ITERS):
        panel = current.astype(jnp.bfloat16)

        def one_block(block_index, gradient):
            start = (block_index * FR_DEV).astype(jnp.int32)
            where_now = lax.dynamic_slice_in_dim(positions, start, FR_DEV, 0)
            measured = lax.dynamic_slice_in_dim(amplitudes, start, FR_DEV, 0)
            windows = cut_windows(panel, where_now[:, 0], where_now[:, 1], M)
            patches = frame_patches(windows, probe_field, measured, tables)
            return place_patches(gradient, patches, where_now[:, 0], where_now[:, 1], weights)
        gradient = lax.fori_loop(0, block_count, one_block, jnp.zeros(current.shape, jnp.float32))
        current = current - STEP_SIZE * gradient
    return current
```

```python
import functools
import math

import jax
import jax.numpy as jnp
import ml_dtypes
import numpy as np
from jax import lax
from jax.experimental import pallas as pl
from jax.experimental.pallas import tpu as pltpu
from jax.sharding import PartitionSpec as P

ITERS = 2
STEP_SIZE = 0.05
AMPLITUDE_FLOOR = 0.25
GROUP = 4


def base_tables(side):
    index = np.arange(side)
    angle = (index[:, None] * index[None, :] % side) * (2.0 * math.pi / side)
    four = np.exp(-1j * angle) / math.sqrt(side)
    centred = (index + side // 2) % side - side // 2
    chirp = np.exp(-1j * math.pi * centred * centred / (4.0 * side))
    first_row = np.array(
        [np.sum(chirp * np.exp(2j * math.pi * index * shift / side)) for shift in range(side)]
    ) / side
    first_row = 0.5 * (first_row + first_row[(-index) % side])
    prop = first_row[(index[:, None] - index[None, :]) % side]
    planes = np.stack([prop.real, prop.imag, four.real, four.imag])
    return planes.astype(ml_dtypes.bfloat16)


def prep_kernel(pos_ref, amp_ref, out_ref, meta_ref, half_ref, src_ref):
    tile_count = lax.axis_size("tile")
    cut_count = lax.axis_size("cuts")
    tile = lax.axis_index("tile")
    cut = lax.axis_index("cuts")
    held = amp_ref.shape[0]
    capacity = out_ref.shape[0] // tile_count
    total = pos_ref.shape[0] // 2
    load = 2 * held
    width = amp_ref.shape[-1]
    for frame in range(held):
        half_ref[frame] = amp_ref[frame].astype(jnp.bfloat16)

    def clear(slot, carry):
        src_ref[slot] = 0
        return carry

    lax.fori_loop(0, out_ref.shape[0], clear, 0)
    start = (tile * cut_count + cut) * held
    owners = [pos_ref[total + start + frame] // width for frame in range(held)]
    for frame in range(held):
        slot = jnp.int32(0)
        for earlier in range(frame):
            slot = slot + (owners[earlier] == owners[frame]).astype(jnp.int32)
        src_ref[owners[frame] * capacity + slot] = frame

    def fill(slot, carry):
        out_ref[slot] = half_ref[src_ref[slot]]
        return carry

    lax.fori_loop(0, out_ref.shape[0], fill, 0)

    def scan(reader, count):
        first = count
        begin = (reader * cut_count + cut) * held
        for frame in range(held):
            col = pos_ref[total + begin + frame]
            meta_ref[count] = pos_ref[begin + frame]
            meta_ref[32 + count] = col - tile * width
            meta_ref[64 + count] = reader * capacity + count - first
            count = count + (col // width == tile).astype(jnp.int32)
        return count

    count = lax.fori_loop(0, tile_count, scan, jnp.int32(0))

    def tidy(slot, carry):
        live = slot < count
        for field in range(3):
            meta_ref[32 * field + slot] = jnp.where(live, meta_ref[32 * field + slot], 0)
        return carry

    lax.fori_loop(0, load, tidy, 0)
    meta_ref[96] = count


def prepare(positions, amplitudes, tile_count, capacity):
    side = amplitudes.shape[-1]
    return pl.pallas_call(
        prep_kernel,
        out_shape=(
            jax.ShapeDtypeStruct((tile_count * capacity, side, side), jnp.bfloat16),
            jax.ShapeDtypeStruct((128,), jnp.int32),
        ),
        in_specs=[
            pl.BlockSpec(memory_space=pltpu.SMEM),
            pl.BlockSpec(memory_space=pltpu.VMEM),
        ],
        out_specs=(
            pl.BlockSpec(memory_space=pltpu.VMEM),
            pl.BlockSpec(memory_space=pltpu.SMEM),
        ),
        scratch_shapes=[
            pltpu.VMEM(amplitudes.shape, jnp.bfloat16),
            pltpu.SMEM((tile_count * capacity,), jnp.int32),
        ],
        name="prep",
    )(positions.T.reshape(-1), amplitudes)


def times(left, right):
    return left[0] * right[0] - left[1] * right[1], left[0] * right[1] + left[1] * right[0]


def conj_times(left, right):
    return left[0] * right[0] + left[1] * right[1], left[0] * right[1] - left[1] * right[0]


def two_sided(fields, right_table, left_table):
    side = fields[0][0].shape[-1]
    results = []
    for pair in range(0, len(fields), 2):
        rows = [
            jnp.concatenate([part.astype(jnp.bfloat16) for part in field], axis=1)
            for field in fields[pair : pair + 2]
        ]
        first = jnp.dot(
            jnp.concatenate(rows, axis=0), right_table, preferred_element_type=jnp.float32
        ).astype(jnp.bfloat16)
        turned = jnp.concatenate(
            [
                jnp.concatenate([first[:side, :side], first[side:, :side]], axis=1),
                jnp.concatenate([first[:side, side:], first[side:, side:]], axis=1),
            ],
            axis=0,
        )
        second = jnp.dot(left_table, turned, preferred_element_type=jnp.float32)
        results.append((second[:side, :side], second[side:, :side]))
        results.append((second[:side, side:], second[side:, side:]))
    return results


def frames_kernel(
    meta_ref, own_ref, next_ref, amp_ref, probe_ref, planes_ref, grad_ref, panel, tables, views, kept
):
    slices = own_ref.shape[0]
    side = own_ref.shape[-1]
    for level in range(slices):
        for part in range(2):
            plane = 2 * level + part
            panel[plane, 0] = own_ref[level, part].astype(jnp.float32)
            panel[plane, 1] = next_ref[level, part].astype(jnp.float32)
    grad_ref[...] = jnp.zeros_like(grad_ref)
    for kind in range(2):
        real, imag = planes_ref[2 * kind], planes_ref[2 * kind + 1]
        tables[2 * kind, :side, :side] = real
        tables[2 * kind, side:, side:] = real
        tables[2 * kind, :side, side:] = imag
        tables[2 * kind, side:, :side] = -imag
        tables[2 * kind + 1, :side, :side] = real
        tables[2 * kind + 1, side:, side:] = real
        tables[2 * kind + 1, :side, side:] = -imag
        tables[2 * kind + 1, side:, :side] = imag
    lane = lax.broadcasted_iota(jnp.int32, (side, side), 1)
    count = meta_ref[96]

    def group_step(group, carry):
        first = group * GROUP
        rows = [meta_ref[first + k] for k in range(GROUP)]
        cols = [meta_ref[32 + first + k] for k in range(GROUP)]
        for k in range(GROUP):
            from_own = lane >= cols[k]
            back_by = (side - cols[k]) % side
            for plane in range(2 * slices):
                joined = jnp.where(
                    from_own,
                    panel[plane, 0, pl.ds(rows[k], side), :],
                    panel[plane, 1, pl.ds(rows[k], side), :],
                )
                views[k, plane] = pltpu.roll(joined, back_by, 1)

        def view(k, level):
            return views[k, 2 * level], views[k, 2 * level + 1]

        def probe():
            return probe_ref[0], probe_ref[1]

        def add(k, level, patch):
            in_own = lane >= cols[k]
            for part in range(2):
                plane = 2 * level + part
                moved = pltpu.roll(patch[part], cols[k], 1)
                where_now = pl.ds(rows[k], side)
                grad_ref[0, plane, where_now, :] += jnp.where(in_own, moved, 0.0)
                grad_ref[1, plane, where_now, :] += jnp.where(in_own, 0.0, moved)

        members = range(GROUP)
        wave = [times(probe(), view(k, 0)) for k in members]
        for level in range(1, slices):
            moved = two_sided(wave, tables[0], tables[1])
            for k in members:
                kept[k, 2 * level - 2] = moved[k][0]
                kept[k, 2 * level - 1] = moved[k][1]
            wave = [times(view(k, level), moved[k]) for k in members]
        far = two_sided(wave, tables[2], tables[3])
        resid = []
        for k in members:
            real, imag = far[k]
            power = jnp.maximum(real * real + imag * imag, AMPLITUDE_FLOOR * AMPLITUDE_FLOOR)
            measured = amp_ref[meta_ref[64 + first + k]].astype(jnp.float32)
            live = jnp.where(first + k < count, 1.0, 0.0)
            factor = live - (live * measured) * lax.rsqrt(power)
            resid.append((real * factor, imag * factor))
        back = two_sided(resid, tables[3], tables[2])
        for level in range(slices - 1, 0, -1):
            for k in members:
                add(k, level, conj_times((kept[k, 2 * level - 2], kept[k, 2 * level - 1]), back[k]))
            back = two_sided(
                [conj_times(view(k, level), back[k]) for k in members], tables[1], tables[0]
            )
        for k in members:
            add(k, 0, conj_times(probe(), back[k]))
        return carry

    lax.fori_loop(0, (count + GROUP - 1) // GROUP, group_step, 0)


def frame_gradient(meta, own, following, measured, probe_field, planes):
    slices, _, height, side = own.shape
    vmem = pl.BlockSpec(memory_space=pltpu.VMEM)
    return pl.pallas_call(
        frames_kernel,
        out_shape=jax.ShapeDtypeStruct((2, 2 * slices, height, side), jnp.float32),
        in_specs=[pl.BlockSpec(memory_space=pltpu.SMEM)] + [vmem] * 5,
        out_specs=vmem,
        scratch_shapes=[
            pltpu.VMEM((2 * slices, 2, height, side), jnp.float32),
            pltpu.VMEM((4, 2 * side, 2 * side), jnp.bfloat16),
            pltpu.VMEM((GROUP, 2 * slices, side, side), jnp.float32),
            pltpu.VMEM((GROUP, 2 * slices - 2, side, side), jnp.float32),
        ],
        compiler_params=pltpu.CompilerParams(vmem_limit_bytes=48 << 20),
        cost_estimate=pl.CostEstimate(
            flops=16 * 16 * 2**24, bytes_accessed=6 << 20, transcendentals=16 * side * side
        ),
        name="frames",
    )(meta, own, following, measured, probe_field, planes)


def passed_along(x, axis, by):
    peers = lax.axis_size(axis)
    pairs = [(i, i + by) for i in range(peers) if 0 <= i + by < peers]
    return lax.ppermute(x, axis, pairs)


def body(amplitudes, positions, probe_field, object_slices):
    tile_count = lax.axis_size("tile")
    frames_held, side, _ = amplitudes.shape
    capacity = max(2, 2 * frames_held // tile_count)
    outgoing, meta = prepare(positions, amplitudes, tile_count, capacity)
    incoming = lax.all_to_all(
        outgoing.reshape(tile_count, capacity, side, side), "tile", split_axis=0, concat_axis=0, tiled=True
    ).reshape(tile_count * capacity, side, side)
    planes = jnp.asarray(base_tables(side))
    current = object_slices
    for turn in range(ITERS):
        stacked = lax.all_gather(current.astype(jnp.bfloat16), "cuts", axis=0, tiled=True)
        following = passed_along(stacked, "tile", -1)
        term = frame_gradient(meta, stacked, following, incoming, probe_field, planes)
        term = term.reshape((2,) + stacked.shape)
        moved = passed_along(term[1], "tile", 1)
        share = lax.psum_scatter(term[0] + moved, "cuts", scatter_dimension=0, tiled=True)
        current = current - STEP_SIZE * share
    return current


def solution(mesh):
    in_specs = (P(("tile", "cuts"), None, None), P(), P(), P("cuts", None, None, "tile"))
    out_specs = P("cuts", None, None, "tile")
    return jax.shard_map(body, mesh=mesh, in_specs=in_specs, out_specs=out_specs, check_vma=False)
```

```python
import functools
import math

import jax
import jax.numpy as jnp
import ml_dtypes
import numpy as np
from jax import lax
from jax.experimental import pallas as pl
from jax.experimental.pallas import tpu as pltpu
from jax.sharding import PartitionSpec as P

ITERS = 2
STEP_SIZE = 0.05
AMPLITUDE_FLOOR = 0.25
GROUP = 4


def base_tables(side):
    index = np.arange(side)
    angle = (index[:, None] * index[None, :] % side) * (2.0 * math.pi / side)
    four = np.exp(-1j * angle) / math.sqrt(side)
    centred = (index + side // 2) % side - side // 2
    chirp = np.exp(-1j * math.pi * centred * centred / (4.0 * side))
    first_row = np.array(
        [np.sum(chirp * np.exp(2j * math.pi * index * shift / side)) for shift in range(side)]
    ) / side
    first_row = 0.5 * (first_row + first_row[(-index) % side])
    prop = first_row[(index[:, None] - index[None, :]) % side]
    planes = np.stack([prop.real, prop.imag, four.real, four.imag])
    return planes.astype(ml_dtypes.bfloat16)


def slots_kernel(pos_ref, amp_ref, out_ref, half_ref, src_ref):
    tile_count = lax.axis_size("tile")
    cut_count = lax.axis_size("cuts")
    held = amp_ref.shape[0]
    capacity = out_ref.shape[0] // tile_count
    total = pos_ref.shape[0] // 2
    shift = amp_ref.shape[-1].bit_length() - 1
    for frame in range(held):
        half_ref[frame] = amp_ref[frame].astype(jnp.bfloat16)
    for slot in range(out_ref.shape[0]):
        src_ref[slot] = 0
    start = (lax.axis_index("tile") * cut_count + lax.axis_index("cuts")) * held
    owners = [pos_ref[total + start + frame] >> shift for frame in range(held)]
    for frame in range(held):
        slot = jnp.int32(0)
        for earlier in range(frame):
            slot = slot + (owners[earlier] == owners[frame]).astype(jnp.int32)
        src_ref[owners[frame] * capacity + slot] = frame
    for slot in range(out_ref.shape[0]):
        out_ref[slot] = half_ref[src_ref[slot]]


def fill_slots(flat_positions, amplitudes, tile_count, capacity):
    side = amplitudes.shape[-1]
    return pl.pallas_call(
        slots_kernel,
        out_shape=jax.ShapeDtypeStruct((tile_count * capacity, side, side), jnp.bfloat16),
        in_specs=[
            pl.BlockSpec(memory_space=pltpu.SMEM),
            pl.BlockSpec(memory_space=pltpu.VMEM),
        ],
        out_specs=pl.BlockSpec(memory_space=pltpu.VMEM),
        scratch_shapes=[
            pltpu.VMEM(amplitudes.shape, jnp.bfloat16),
            pltpu.SMEM((tile_count * capacity,), jnp.int32),
        ],
        name="slots",
    )(flat_positions, amplitudes)


def list_kernel(held, shift, capacity, pos_ref, meta_ref):
    tile_count = lax.axis_size("tile")
    cut_count = lax.axis_size("cuts")
    tile = lax.axis_index("tile")
    cut = lax.axis_index("cuts")
    total = pos_ref.shape[0] // 2
    load = 2 * held

    def scan(reader, count):
        begin = (reader * cut_count + cut) * held
        for frame in range(held):
            meta_ref[64 + count] = reader * held + frame
            count = count + ((pos_ref[total + begin + frame] >> shift) == tile).astype(jnp.int32)
        return count

    count = lax.fori_loop(0, tile_count, scan, jnp.int32(0))
    before, slot = jnp.int32(-1), jnp.int32(0)
    for rank in range(load):
        live = rank < count
        packed = jnp.where(live, meta_ref[64 + rank], 0)
        reader = packed // held
        frame = reader * cut_count * held + cut * held + packed % held
        slot = jnp.where(reader == before, slot + 1, 0)
        before = reader
        meta_ref[rank] = jnp.where(live, pos_ref[frame], 0)
        meta_ref[32 + rank] = jnp.where(live, pos_ref[total + frame] - (tile << shift), 0)
        meta_ref[64 + rank] = jnp.where(live, reader * capacity + slot, 0)
    meta_ref[96] = count


def list_frames(flat_positions, held, side, capacity):
    return pl.pallas_call(
        functools.partial(list_kernel, held, side.bit_length() - 1, capacity),
        out_shape=jax.ShapeDtypeStruct((128,), jnp.int32),
        in_specs=[pl.BlockSpec(memory_space=pltpu.SMEM)],
        out_specs=pl.BlockSpec(memory_space=pltpu.SMEM),
        name="listing",
    )(flat_positions)


def exchange_kernel(reduces, gathers, *refs):
    refs = list(refs)
    term_ref = refs.pop(0) if reduces else None
    held_ref = refs.pop(0)
    new_ref = refs.pop(0) if reduces else None
    own_ref, next_ref = (refs.pop(0), refs.pop(0)) if gathers else (None, None)
    if reduces:
        out_box, in_box, far_out, far_in, near_out, near_in = refs[:6]
        tile_send, tile_recv, cut_send, cut_recv = refs[6:10]
        refs = refs[10:]
    if gathers:
        rim_send, rim_recv, ring_send, ring_recv = refs
    tile_count = lax.axis_size("tile")
    tile = lax.axis_index("tile")
    me = lax.axis_index("cuts")
    peers = 4
    right, left, across = (me + 1) % peers, (me + 3) % peers, (me + 2) % peers
    has_next = tile < tile_count - 1
    has_prev = tile > 0
    barrier = pltpu.get_barrier_semaphore()

    def greet(to_tile, to_cut):
        pl.semaphore_signal(
            barrier,
            inc=1,
            device_id={"tile": to_tile, "cuts": to_cut},
            device_id_type=pl.DeviceIdType.MESH,
        )

    greet(tile, right)
    greet(tile, left)

    @pl.when(has_next)
    def _():
        greet(tile + 1, me)

    @pl.when(has_prev)
    def _():
        greet(tile - 1, me)

    def to_cut(source, target, sends, recvs, index, cut):
        return pltpu.make_async_remote_copy(
            src_ref=source,
            dst_ref=target,
            send_sem=sends.at[index],
            recv_sem=recvs.at[index],
            device_id={"tile": tile, "cuts": cut},
            device_id_type=pl.DeviceIdType.MESH,
        )

    def to_tile(source, target, sends, recvs, index, by):
        return pltpu.make_async_remote_copy(
            src_ref=source,
            dst_ref=target,
            send_sem=sends.at[index],
            recv_sem=recvs.at[index],
            device_id={"tile": tile + by, "cuts": me},
            device_id_type=pl.DeviceIdType.MESH,
        )

    def all_arrived():
        pl.semaphore_wait(barrier, 2 + has_next.astype(jnp.int32) + has_prev.astype(jnp.int32))

    def plane(half, level, part):
        return term_ref[half, 2 * level + part]

    if reduces:
        order = [across, right, left, me]
        forward = [
            to_tile(out_box.at[k], in_box.at[k], tile_send, tile_recv, k, 1) for k in range(peers)
        ]

        @pl.when(has_next)
        def _():
            for k in range(peers):
                for part in range(2):
                    out_box[k, part] = plane(1, order[k], part).astype(jnp.bfloat16)

        @pl.when(jnp.logical_not(has_prev))
        def _():
            in_box[...] = jnp.zeros_like(in_box)

        all_arrived()

        @pl.when(has_next)
        def _():
            for copy in forward:
                copy.start()

        def arrived(k):
            @pl.when(has_prev)
            def _():
                forward[k].wait_recv()

        def joined(k, part):
            return plane(0, order[k], part) + in_box[k, part].astype(jnp.float32)

        arrived(0)
        far_out[0] = joined(0, 0).astype(jnp.bfloat16)
        far_out[1] = joined(0, 1).astype(jnp.bfloat16)
        far_right = to_cut(far_out.at[0], far_in.at[0], cut_send, cut_recv, 0, right)
        far_left = to_cut(far_out.at[1], far_in.at[1], cut_send, cut_recv, 1, left)
        far_right.start()
        far_left.start()
        near_right = to_cut(near_out.at[0], near_in.at[0], cut_send, cut_recv, 2, right)
        near_left = to_cut(near_out.at[1], near_in.at[1], cut_send, cut_recv, 3, left)
        arrived(1)
        near_out[0, 1] = joined(1, 1).astype(jnp.bfloat16)
        far_right.wait_recv()
        near_out[0, 0] = (joined(1, 0) + far_in[0].astype(jnp.float32)).astype(jnp.bfloat16)
        near_right.start()
        arrived(2)
        near_out[1, 0] = joined(2, 0).astype(jnp.bfloat16)
        far_left.wait_recv()
        near_out[1, 1] = (joined(2, 1) + far_in[1].astype(jnp.float32)).astype(jnp.bfloat16)
        near_left.start()
        arrived(3)
        for part in range(2):
            new_ref[0, part] = joined(3, part)
        near_right.wait_recv()
        near_left.wait_recv()
        for part in range(2):
            share = (
                new_ref[0, part]
                + near_in[0, part].astype(jnp.float32)
                + near_in[1, part].astype(jnp.float32)
            )
            fresh = held_ref[0, part] - STEP_SIZE * share
            new_ref[0, part] = fresh
            if gathers:
                own_ref[me, part] = fresh.astype(jnp.bfloat16)
    else:
        for part in range(2):
            own_ref[me, part] = held_ref[0, part].astype(jnp.bfloat16)
        all_arrived()

    if gathers:

        def ring(index, level, part, cut):
            spot = own_ref.at[level] if part is None else own_ref.at[level, part]
            return to_cut(spot, spot, ring_send, ring_recv, index, cut)

        def rim(index, level):
            return to_tile(own_ref.at[level], next_ref.at[level], rim_send, rim_recv, index, -1)

        go_right, go_left = ring(0, me, None, right), ring(1, me, None, left)
        from_left, from_right = ring(0, left, None, right), ring(1, right, None, left)
        on_right, on_left = ring(2, left, 0, right), ring(3, right, 1, left)
        far_first, far_second = ring(2, across, 0, right), ring(3, across, 1, left)
        rims = [rim(0, me), rim(1, left), rim(2, right), rim(3, across)]

        def pass_rim(k):
            @pl.when(has_prev)
            def _():
                rims[k].start()

        go_right.start()
        go_left.start()
        pass_rim(0)
        from_left.wait_recv()
        on_right.start()
        pass_rim(1)
        from_right.wait_recv()
        on_left.start()
        pass_rim(2)
        far_first.wait_recv()
        far_second.wait_recv()
        pass_rim(3)

        @pl.when(has_next)
        def _():
            for copy in rims:
                copy.wait_recv()

        @pl.when(jnp.logical_not(has_next))
        def _():
            next_ref[...] = jnp.zeros_like(next_ref)

        for copy in (go_right, go_left, on_right, on_left):
            copy.wait_send()

        @pl.when(has_prev)
        def _():
            for copy in rims:
                copy.wait_send()

    if reduces:
        for copy in (far_right, far_left, near_right, near_left):
            copy.wait_send()

        @pl.when(has_next)
        def _():
            for copy in forward:
                copy.wait_send()


def exchange(term, held, gathers, number):
    reduces = term is not None
    _, parts, height, width = held.shape
    peers = lax.axis_size("cuts")
    slices = peers
    vmem = pl.BlockSpec(memory_space=pltpu.VMEM)
    outs, scratch = [], []
    if reduces:
        outs.append(jax.ShapeDtypeStruct(held.shape, jnp.float32))
        scratch += [
            pltpu.VMEM((peers, parts, height, width), jnp.bfloat16),
            pltpu.VMEM((peers, parts, height, width), jnp.bfloat16),
            pltpu.VMEM((2, height, width), jnp.bfloat16),
            pltpu.VMEM((2, height, width), jnp.bfloat16),
            pltpu.VMEM((2, parts, height, width), jnp.bfloat16),
            pltpu.VMEM((2, parts, height, width), jnp.bfloat16),
        ] + [pltpu.SemaphoreType.DMA((4,))] * 4
    if gathers:
        outs += [jax.ShapeDtypeStruct((slices, parts, height, width), jnp.bfloat16)] * 2
        scratch += [pltpu.SemaphoreType.DMA((4,))] * 4
    operands = ([term] if reduces else []) + [held]
    return pl.pallas_call(
        functools.partial(exchange_kernel, reduces, gathers),
        out_shape=tuple(outs),
        in_specs=[vmem] * len(operands),
        out_specs=tuple([vmem] * len(outs)),
        scratch_shapes=scratch,
        compiler_params=pltpu.CompilerParams(
            collective_id=number, has_side_effects=True, vmem_limit_bytes=40 << 20
        ),
        name="exchange",
    )(*operands)


def times(left, right):
    return left[0] * right[0] - left[1] * right[1], left[0] * right[1] + left[1] * right[0]


def conj_times(left, right):
    return left[0] * right[0] + left[1] * right[1], left[0] * right[1] - left[1] * right[0]


def two_sided(fields, right_table, left_table):
    side = fields[0][0].shape[-1]
    results = []
    for pair in range(0, len(fields), 2):
        rows = [
            jnp.concatenate([part.astype(jnp.bfloat16) for part in field], axis=1)
            for field in fields[pair : pair + 2]
        ]
        first = jnp.dot(
            jnp.concatenate(rows, axis=0), right_table, preferred_element_type=jnp.float32
        ).astype(jnp.bfloat16)
        turned = jnp.concatenate(
            [
                jnp.concatenate([first[:side, :side], first[side:, :side]], axis=1),
                jnp.concatenate([first[:side, side:], first[side:, side:]], axis=1),
            ],
            axis=0,
        )
        second = jnp.dot(left_table, turned, preferred_element_type=jnp.float32)
        results.append((second[:side, :side], second[side:, :side]))
        results.append((second[:side, side:], second[side:, side:]))
    return results


def frames_kernel(
    meta_ref, own_ref, next_ref, amp_ref, probe_ref, planes_ref, grad_ref, panel, tables, views, kept
):
    slices = own_ref.shape[0]
    side = own_ref.shape[-1]
    for level in range(slices):
        for part in range(2):
            plane = 2 * level + part
            panel[plane, 0] = own_ref[level, part].astype(jnp.float32)
            panel[plane, 1] = next_ref[level, part].astype(jnp.float32)
    grad_ref[...] = jnp.zeros_like(grad_ref)
    for kind in range(2):
        real, imag = planes_ref[2 * kind], planes_ref[2 * kind + 1]
        tables[2 * kind, :side, :side] = real
        tables[2 * kind, side:, side:] = real
        tables[2 * kind, :side, side:] = imag
        tables[2 * kind, side:, :side] = -imag
        tables[2 * kind + 1, :side, :side] = real
        tables[2 * kind + 1, side:, side:] = real
        tables[2 * kind + 1, :side, side:] = -imag
        tables[2 * kind + 1, side:, :side] = imag
    lane = lax.broadcasted_iota(jnp.int32, (side, side), 1)
    count = meta_ref[96]

    def group_step(group, carry):
        first = group * GROUP
        rows = [meta_ref[first + k] for k in range(GROUP)]
        cols = [meta_ref[32 + first + k] for k in range(GROUP)]
        for k in range(GROUP):
            from_own = lane >= cols[k]
            back_by = (side - cols[k]) % side
            for plane in range(2 * slices):
                joined = jnp.where(
                    from_own,
                    panel[plane, 0, pl.ds(rows[k], side), :],
                    panel[plane, 1, pl.ds(rows[k], side), :],
                )
                views[k, plane] = pltpu.roll(joined, back_by, 1)

        def view(k, level):
            return views[k, 2 * level], views[k, 2 * level + 1]

        def probe():
            return probe_ref[0], probe_ref[1]

        def add(k, level, patch):
            in_own = lane >= cols[k]
            for part in range(2):
                plane = 2 * level + part
                moved = pltpu.roll(patch[part], cols[k], 1)
                where_now = pl.ds(rows[k], side)
                grad_ref[0, plane, where_now, :] += jnp.where(in_own, moved, 0.0)
                grad_ref[1, plane, where_now, :] += jnp.where(in_own, 0.0, moved)

        members = range(GROUP)
        wave = [times(probe(), view(k, 0)) for k in members]
        for level in range(1, slices):
            moved = two_sided(wave, tables[0], tables[1])
            for k in members:
                kept[k, 2 * level - 2] = moved[k][0]
                kept[k, 2 * level - 1] = moved[k][1]
            wave = [times(view(k, level), moved[k]) for k in members]
        far = two_sided(wave, tables[2], tables[3])
        resid = []
        for k in members:
            real, imag = far[k]
            power = jnp.maximum(real * real + imag * imag, AMPLITUDE_FLOOR * AMPLITUDE_FLOOR)
            measured = amp_ref[meta_ref[64 + first + k]].astype(jnp.float32)
            live = jnp.where(first + k < count, 1.0, 0.0)
            factor = live - (live * measured) * lax.rsqrt(power)
            resid.append((real * factor, imag * factor))
        back = two_sided(resid, tables[3], tables[2])
        for level in range(slices - 1, 0, -1):
            for k in members:
                add(k, level, conj_times((kept[k, 2 * level - 2], kept[k, 2 * level - 1]), back[k]))
            back = two_sided(
                [conj_times(view(k, level), back[k]) for k in members], tables[1], tables[0]
            )
        for k in members:
            add(k, 0, conj_times(probe(), back[k]))
        return carry

    lax.fori_loop(0, (count + GROUP - 1) // GROUP, group_step, 0)


def frame_gradient(meta, own, following, measured, probe_field, planes):
    slices, _, height, side = own.shape
    vmem = pl.BlockSpec(memory_space=pltpu.VMEM)
    return pl.pallas_call(
        frames_kernel,
        out_shape=jax.ShapeDtypeStruct((2, 2 * slices, height, side), jnp.float32),
        in_specs=[pl.BlockSpec(memory_space=pltpu.SMEM)] + [vmem] * 5,
        out_specs=vmem,
        scratch_shapes=[
            pltpu.VMEM((2 * slices, 2, height, side), jnp.float32),
            pltpu.VMEM((4, 2 * side, 2 * side), jnp.bfloat16),
            pltpu.VMEM((GROUP, 2 * slices, side, side), jnp.float32),
            pltpu.VMEM((GROUP, 2 * slices - 2, side, side), jnp.float32),
        ],
        compiler_params=pltpu.CompilerParams(vmem_limit_bytes=48 << 20),
        cost_estimate=pl.CostEstimate(
            flops=16 * 16 * 2**24, bytes_accessed=6 << 20, transcendentals=16 * side * side
        ),
        name="frames",
    )(meta, own, following, measured, probe_field, planes)


def body(amplitudes, positions, probe_field, object_slices):
    tile_count = lax.axis_size("tile")
    frames_held, side, _ = amplitudes.shape
    capacity = max(2, 2 * frames_held // tile_count)
    flat_positions = positions.T.reshape(-1)
    outgoing = fill_slots(flat_positions, amplitudes, tile_count, capacity)
    incoming = lax.all_to_all(
        outgoing.reshape(tile_count, capacity, side, side), "tile", split_axis=0, concat_axis=0, tiled=True
    ).reshape(tile_count * capacity, side, side)
    meta = list_frames(flat_positions, frames_held, side, capacity)
    planes = jnp.asarray(base_tables(side))
    own, following = exchange(None, object_slices, True, 1)
    current = object_slices
    for turn in range(ITERS):
        term = frame_gradient(meta, own, following, incoming, probe_field, planes)
        if turn < ITERS - 1:
            current, own, following = exchange(term, current, True, 2 + turn)
        else:
            (current,) = exchange(term, current, False, 2 + turn)
    return current


def solution(mesh):
    in_specs = (P(("tile", "cuts"), None, None), P(), P(), P("cuts", None, None, "tile"))
    out_specs = P("cuts", None, None, "tile")
    return jax.shard_map(body, mesh=mesh, in_specs=in_specs, out_specs=out_specs, check_vma=False)
```

```python
import functools
import math

import jax
import jax.numpy as jnp
import ml_dtypes
import numpy as np
from jax import lax
from jax.experimental import pallas as pl
from jax.experimental.pallas import tpu as pltpu
from jax.sharding import PartitionSpec as P

ITERS = 2
STEP_SIZE = 0.05
AMPLITUDE_FLOOR = 0.25
GROUP = 8
RING = 4


def base_tables(side):
    index = np.arange(side)
    angle = (index[:, None] * index[None, :] % side) * (2.0 * math.pi / side)
    four = np.exp(-1j * angle) / math.sqrt(side)
    centred = (index + side // 2) % side - side // 2
    chirp = np.exp(-1j * math.pi * centred * centred / (4.0 * side))
    first_row = np.array(
        [np.sum(chirp * np.exp(2j * math.pi * index * shift / side)) for shift in range(side)]
    ) / side
    first_row = 0.5 * (first_row + first_row[(-index) % side])
    prop = first_row[(index[:, None] - index[None, :]) % side]
    planes = np.stack([prop.real, prop.imag, four.real, four.imag])
    return planes.astype(ml_dtypes.bfloat16)


def list_kernel(held, shift, capacity, pos_ref, meta_ref):
    tile_count = lax.axis_size("tile")
    cut_count = lax.axis_size("cuts")
    tile = lax.axis_index("tile")
    cut = lax.axis_index("cuts")
    total = pos_ref.shape[0] // 2
    load = 2 * held

    def scan(reader, count):
        begin = (reader * cut_count + cut) * held
        for frame in range(held):
            meta_ref[64 + count] = reader * held + frame
            count = count + ((pos_ref[total + begin + frame] >> shift) == tile).astype(jnp.int32)
        return count

    count = lax.fori_loop(0, tile_count, scan, jnp.int32(0))
    before, slot = jnp.int32(-1), jnp.int32(0)
    for rank in range(load):
        live = rank < count
        packed = jnp.where(live, meta_ref[64 + rank], 0)
        reader = packed // held
        frame = reader * cut_count * held + cut * held + packed % held
        slot = jnp.where(reader == before, slot + 1, 0)
        before = reader
        meta_ref[rank] = jnp.where(live, pos_ref[frame], 0)
        meta_ref[32 + rank] = jnp.where(live, pos_ref[total + frame] - (tile << shift), 0)
        core, along_z, along_x = reader % 2, reader // 2 % RING, reader // (2 * RING)
        line = jnp.where(core == 0, along_z * RING + along_x, (RING + along_x) * RING + along_z)
        meta_ref[64 + rank] = jnp.where(live, line * capacity + slot, 0)
    meta_ref[96] = count


def list_frames(flat_positions, held, side, capacity):
    return pl.pallas_call(
        functools.partial(list_kernel, held, side.bit_length() - 1, capacity),
        out_shape=jax.ShapeDtypeStruct((128,), jnp.int32),
        in_specs=[pl.BlockSpec(memory_space=pltpu.SMEM)],
        out_specs=pl.BlockSpec(memory_space=pltpu.SMEM),
        name="listing",
    )(flat_positions)


def mesh_copy(source, target, send, recv, tile, cut):
    return pltpu.make_async_remote_copy(
        src_ref=source,
        dst_ref=target,
        send_sem=send,
        recv_sem=recv,
        device_id={"tile": tile, "cuts": cut},
        device_id_type=pl.DeviceIdType.MESH,
    )


def greet(barrier, tile, cut):
    pl.semaphore_signal(
        barrier,
        inc=1,
        device_id={"tile": tile, "cuts": cut},
        device_id_type=pl.DeviceIdType.MESH,
    )


def greet_near(barrier):
    tile_count = lax.axis_size("tile")
    tile = lax.axis_index("tile")
    me = lax.axis_index("cuts")
    has_next = tile < tile_count - 1
    has_prev = tile > 0
    greet(barrier, tile, (me + 1) % RING)
    greet(barrier, tile, (me + 3) % RING)

    @pl.when(has_next)
    def _():
        greet(barrier, tile + 1, me)

    @pl.when(has_prev)
    def _():
        greet(barrier, tile - 1, me)

    return 2 + has_next.astype(jnp.int32) + has_prev.astype(jnp.int32)


def gather_steps(own_ref, next_ref, rim_send, rim_recv, ring_send, ring_recv):
    tile_count = lax.axis_size("tile")
    tile = lax.axis_index("tile")
    me = lax.axis_index("cuts")
    right, left, across = (me + 1) % RING, (me + 3) % RING, (me + 2) % RING
    has_next = tile < tile_count - 1
    has_prev = tile > 0

    def ring(index, level, part, cut):
        spot = own_ref.at[level] if part is None else own_ref.at[level, part]
        return mesh_copy(spot, spot, ring_send.at[index], ring_recv.at[index], tile, cut)

    def rim(index, level):
        return mesh_copy(
            own_ref.at[level], next_ref.at[level], rim_send.at[index], rim_recv.at[index], tile - 1, me
        )

    go_right, go_left = ring(0, me, None, right), ring(1, me, None, left)
    from_left, from_right = ring(0, left, None, right), ring(1, right, None, left)
    on_right, on_left = ring(2, left, 0, right), ring(3, right, 1, left)
    far_first, far_second = ring(2, across, 0, right), ring(3, across, 1, left)
    rims = [rim(0, me), rim(1, left), rim(2, right), rim(3, across)]

    def pass_rim(k):
        @pl.when(has_prev)
        def _():
            rims[k].start()

    def begin():
        go_right.start()
        go_left.start()
        pass_rim(0)

    def take_left():
        from_left.wait_recv()
        on_right.start()
        pass_rim(1)

    def take_right():
        from_right.wait_recv()
        on_left.start()
        pass_rim(2)

    def take_across():
        far_first.wait_recv()
        far_second.wait_recv()
        pass_rim(3)

    def finish():
        @pl.when(has_next)
        def _():
            for copy in rims:
                copy.wait_recv()

        @pl.when(jnp.logical_not(has_next))
        def _():
            next_ref[...] = jnp.zeros_like(next_ref)

        for copy in (go_right, go_left, on_right, on_left):
            copy.wait_send()

        @pl.when(has_prev)
        def _():
            for copy in rims:
                copy.wait_send()

    return begin, take_left, take_right, take_across, finish


def opening_kernel(
    pos_ref, amp_ref, held_ref, own_ref, next_ref, inbox, mine, below, above, far, outbox,
    line_send, line_recv, box_send, box_recv, rim_send, rim_recv, ring_send, ring_recv,
):
    cut_count = lax.axis_size("cuts")
    tile = lax.axis_index("tile")
    me = lax.axis_index("cuts")
    held, side, _ = amp_ref.shape
    shift = side.bit_length() - 1
    total = pos_ref.shape[0] // 2
    core = tile % 2
    along_z = tile // 2 % RING
    along_x = tile // (2 * RING)
    first = (1 - core) * along_x + core * along_z
    second = (1 - core) * along_z + core * along_x

    def tile_at(first_at, second_at, target_core):
        chip = (1 - core) * (first_at * RING + second_at) + core * (second_at * RING + first_at)
        return chip * 2 + target_core

    barrier = pltpu.get_barrier_semaphore()
    expected = greet_near(barrier)
    greet(barrier, tile_at(first, second, 1 - core), me)
    for by in range(1, RING):
        for target_core in range(2):
            greet(barrier, tile_at((first + by) % RING, second, target_core), me)
            greet(barrier, tile_at(first, (second + by) % RING, target_core), me)
            expected = expected + 2
    for part in range(2):
        own_ref[me, part] = held_ref[0, part].astype(jnp.bfloat16)
    for frame in range(held):
        mine[frame] = amp_ref[frame].astype(jnp.bfloat16)
    pl.semaphore_wait(barrier, expected + 1)

    half = held // 2

    def pass_on(index, source, target, begin, count, by):
        return mesh_copy(
            source.at[pl.ds(begin, count)],
            target.at[pl.ds(begin, count)],
            line_send.at[index],
            line_recv.at[index],
            tile_at((first + by) % RING, second, core),
            me,
        )

    before, after, beyond = (first + 3) % RING, (first + 1) % RING, (first + 2) % RING
    go_up, go_down = pass_on(0, mine, below, 0, held, 1), pass_on(1, mine, above, 0, held, 3)
    on_up, on_down = pass_on(2, below, far, 0, half, 1), pass_on(3, above, far, half, half, 3)

    sent = []

    def deal(order, place, line):
        reader = tile_at(place, second, core) * cut_count + me
        owners = [pos_ref[total + reader * held + frame] >> shift for frame in range(held)]
        for target, (by, swap) in enumerate(
            [(2, 0), (2, 1), (1, 0), (3, 0), (1, 1), (3, 1), (0, 1), (0, 0)]
        ):
            target_core = core if swap == 0 else 1 - core
            goal = tile_at(first, (second + by) % RING, target_core)
            seen = jnp.int32(0)
            pick = [jnp.int32(0), jnp.int32(0)]
            for frame in range(held):
                hit = owners[frame] == goal
                pick[1] = jnp.where(jnp.logical_and(hit, seen == 1), frame, pick[1])
                pick[0] = jnp.where(jnp.logical_and(hit, seen == 0), frame, pick[0])
                seen = seen + hit.astype(jnp.int32)
            for slot in range(2):
                if by == 0 and swap == 0:
                    inbox[core, second, place, slot] = line[pick[slot]]
                else:
                    outbox[order, target, slot] = line[pick[slot]]
            if by or swap:
                copy = mesh_copy(
                    outbox.at[order, target],
                    inbox.at[core, second, place],
                    box_send.at[order, target],
                    box_recv.at[core, second, place],
                    goal,
                    me,
                )
                copy.start()
                sent.append(copy)

    begin, take_left, take_right, take_across, finish = gather_steps(
        own_ref, next_ref, rim_send, rim_recv, ring_send, ring_recv
    )
    begin()
    go_up.start()
    go_down.start()
    deal(0, first, mine)
    take_left()
    take_right()
    go_up.wait_recv()
    on_up.start()
    deal(1, before, below)
    take_across()
    go_down.wait_recv()
    on_down.start()
    deal(2, after, above)
    on_up.wait_recv()
    on_down.wait_recv()
    deal(3, beyond, far)
    finish()
    for sender_core, sender_second in [(core, (second + by) % RING) for by in range(1, RING)] + [
        (1 - core, at) for at in range(RING)
    ]:
        for place in range(RING):
            mesh_copy(
                outbox.at[0, 0],
                inbox.at[sender_core, sender_second, place],
                box_send.at[0, 0],
                box_recv.at[sender_core, sender_second, place],
                tile_at(first, second, 1 - core),
                me,
            ).wait_recv()
    for copy in [go_up, go_down, on_up, on_down] + sent:
        copy.wait_send()


def opening(flat_positions, amplitudes, held):
    frames_held, side, _ = amplitudes.shape
    _, parts, height, width = held.shape
    vmem = pl.BlockSpec(memory_space=pltpu.VMEM)
    panel = jax.ShapeDtypeStruct((RING, parts, height, width), jnp.bfloat16)
    own, following, inbox = pl.pallas_call(
        opening_kernel,
        out_shape=(
            panel,
            panel,
            jax.ShapeDtypeStruct((2, RING, RING, 2, side, side), jnp.bfloat16),
        ),
        in_specs=[pl.BlockSpec(memory_space=pltpu.SMEM), vmem, vmem],
        out_specs=(vmem, vmem, vmem),
        scratch_shapes=[
            *[pltpu.VMEM((frames_held, side, side), jnp.bfloat16)] * 4,
            pltpu.VMEM((RING, 7, 2, side, side), jnp.bfloat16),
            pltpu.SemaphoreType.DMA((4,)),
            pltpu.SemaphoreType.DMA((4,)),
            pltpu.SemaphoreType.DMA((RING, 7)),
            pltpu.SemaphoreType.DMA((2, RING, RING)),
        ]
        + [pltpu.SemaphoreType.DMA((4,))] * 4,
        compiler_params=pltpu.CompilerParams(
            collective_id=1, has_side_effects=True, vmem_limit_bytes=40 << 20
        ),
        name="opening",
    )(flat_positions, amplitudes, held)
    return own, following, inbox.reshape(-1, side, side)


def exchange_kernel(gathers, term_ref, held_ref, new_ref, *refs):
    own_ref, next_ref = refs[:2] if gathers else (None, None)
    refs = refs[2:] if gathers else refs
    out_box, in_box, far_out, far_in, near_out, near_in = refs[:6]
    tile_send, tile_recv, cut_send, cut_recv = refs[6:10]
    tile_count = lax.axis_size("tile")
    tile = lax.axis_index("tile")
    me = lax.axis_index("cuts")
    peers = RING
    right, left, across = (me + 1) % peers, (me + 3) % peers, (me + 2) % peers
    has_next = tile < tile_count - 1
    has_prev = tile > 0
    barrier = pltpu.get_barrier_semaphore()
    expected = greet_near(barrier)

    def to_cut(source, target, sends, recvs, index, cut):
        return mesh_copy(source, target, sends.at[index], recvs.at[index], tile, cut)

    def to_tile(source, target, sends, recvs, index, by):
        return mesh_copy(source, target, sends.at[index], recvs.at[index], tile + by, me)

    def plane(half, level, part):
        return term_ref[half, 2 * level + part]

    order = [across, right, left, me]
    forward = [
        to_tile(out_box.at[k], in_box.at[k], tile_send, tile_recv, k, 1) for k in range(peers)
    ]

    @pl.when(has_next)
    def _():
        for k in range(peers):
            for part in range(2):
                out_box[k, part] = plane(1, order[k], part).astype(jnp.bfloat16)

    @pl.when(jnp.logical_not(has_prev))
    def _():
        in_box[...] = jnp.zeros_like(in_box)

    pl.semaphore_wait(barrier, expected)

    @pl.when(has_next)
    def _():
        for copy in forward:
            copy.start()

    def arrived(k):
        @pl.when(has_prev)
        def _():
            forward[k].wait_recv()

    def joined(k, part):
        return plane(0, order[k], part) + in_box[k, part].astype(jnp.float32)

    arrived(0)
    far_out[0] = joined(0, 0).astype(jnp.bfloat16)
    far_out[1] = joined(0, 1).astype(jnp.bfloat16)
    far_right = to_cut(far_out.at[0], far_in.at[0], cut_send, cut_recv, 0, right)
    far_left = to_cut(far_out.at[1], far_in.at[1], cut_send, cut_recv, 1, left)
    far_right.start()
    far_left.start()
    near_right = to_cut(near_out.at[0], near_in.at[0], cut_send, cut_recv, 2, right)
    near_left = to_cut(near_out.at[1], near_in.at[1], cut_send, cut_recv, 3, left)
    arrived(1)
    near_out[0, 1] = joined(1, 1).astype(jnp.bfloat16)
    far_right.wait_recv()
    near_out[0, 0] = (joined(1, 0) + far_in[0].astype(jnp.float32)).astype(jnp.bfloat16)
    near_right.start()
    arrived(2)
    near_out[1, 0] = joined(2, 0).astype(jnp.bfloat16)
    far_left.wait_recv()
    near_out[1, 1] = (joined(2, 1) + far_in[1].astype(jnp.float32)).astype(jnp.bfloat16)
    near_left.start()
    arrived(3)
    for part in range(2):
        new_ref[0, part] = joined(3, part)
    near_right.wait_recv()
    near_left.wait_recv()
    for part in range(2):
        share = (
            new_ref[0, part]
            + near_in[0, part].astype(jnp.float32)
            + near_in[1, part].astype(jnp.float32)
        )
        fresh = held_ref[0, part] - STEP_SIZE * share
        new_ref[0, part] = fresh
        if gathers:
            own_ref[me, part] = fresh.astype(jnp.bfloat16)

    if gathers:
        for step in gather_steps(own_ref, next_ref, *refs[10:]):
            step()

    for copy in (far_right, far_left, near_right, near_left):
        copy.wait_send()

    @pl.when(has_next)
    def _():
        for copy in forward:
            copy.wait_send()


def exchange(term, held, gathers, number):
    _, parts, height, width = held.shape
    vmem = pl.BlockSpec(memory_space=pltpu.VMEM)
    outs = [jax.ShapeDtypeStruct(held.shape, jnp.float32)]
    scratch = [
        pltpu.VMEM((RING, parts, height, width), jnp.bfloat16),
        pltpu.VMEM((RING, parts, height, width), jnp.bfloat16),
        pltpu.VMEM((2, height, width), jnp.bfloat16),
        pltpu.VMEM((2, height, width), jnp.bfloat16),
        pltpu.VMEM((2, parts, height, width), jnp.bfloat16),
        pltpu.VMEM((2, parts, height, width), jnp.bfloat16),
    ] + [pltpu.SemaphoreType.DMA((4,))] * 4
    if gathers:
        outs += [jax.ShapeDtypeStruct((RING, parts, height, width), jnp.bfloat16)] * 2
        scratch += [pltpu.SemaphoreType.DMA((4,))] * 4
    return pl.pallas_call(
        functools.partial(exchange_kernel, gathers),
        out_shape=tuple(outs),
        in_specs=[vmem] * 2,
        out_specs=tuple([vmem] * len(outs)),
        scratch_shapes=scratch,
        compiler_params=pltpu.CompilerParams(
            collective_id=number, has_side_effects=True, vmem_limit_bytes=40 << 20
        ),
        name="exchange",
    )(term, held)


def times(left, right):
    return left[0] * right[0] - left[1] * right[1], left[0] * right[1] + left[1] * right[0]


def conj_times(left, right):
    return left[0] * right[0] + left[1] * right[1], left[0] * right[1] - left[1] * right[0]


def two_sided(fields, right_table, left_table):
    side = fields[0][0].shape[-1]
    results = []
    for pair in range(0, len(fields), 2):
        rows = [
            jnp.concatenate([part.astype(jnp.bfloat16) for part in field], axis=1)
            for field in fields[pair : pair + 2]
        ]
        first = jnp.dot(
            jnp.concatenate(rows, axis=0), right_table, preferred_element_type=jnp.float32
        ).astype(jnp.bfloat16)
        turned = jnp.concatenate(
            [
                jnp.concatenate([first[:side, :side], first[side:, :side]], axis=1),
                jnp.concatenate([first[:side, side:], first[side:, side:]], axis=1),
            ],
            axis=0,
        )
        second = jnp.dot(left_table, turned, preferred_element_type=jnp.float32)
        results.append((second[:side, :side], second[side:, :side]))
        results.append((second[:side, side:], second[side:, side:]))
    return results


def frames_kernel(
    meta_ref, own_ref, next_ref, amp_ref, probe_ref, planes_ref, grad_ref, panel, tables, views, kept
):
    slices = own_ref.shape[0]
    side = own_ref.shape[-1]
    for level in range(slices):
        for part in range(2):
            plane = 2 * level + part
            panel[plane, 0] = own_ref[level, part].astype(jnp.float32)
            panel[plane, 1] = next_ref[level, part].astype(jnp.float32)
    grad_ref[...] = jnp.zeros_like(grad_ref)
    for kind in range(2):
        real, imag = planes_ref[2 * kind], planes_ref[2 * kind + 1]
        tables[2 * kind, :side, :side] = real
        tables[2 * kind, side:, side:] = real
        tables[2 * kind, :side, side:] = imag
        tables[2 * kind, side:, :side] = -imag
        tables[2 * kind + 1, :side, :side] = real
        tables[2 * kind + 1, side:, side:] = real
        tables[2 * kind + 1, :side, side:] = -imag
        tables[2 * kind + 1, side:, :side] = imag
    lane = lax.broadcasted_iota(jnp.int32, (side, side), 1)
    count = meta_ref[96]

    def group_step(group, carry):
        first = group * GROUP
        rows = [meta_ref[first + k] for k in range(GROUP)]
        cols = [meta_ref[32 + first + k] for k in range(GROUP)]
        for k in range(GROUP):
            from_own = lane >= cols[k]
            back_by = (side - cols[k]) % side
            for plane in range(2 * slices):
                joined = jnp.where(
                    from_own,
                    panel[plane, 0, pl.ds(rows[k], side), :],
                    panel[plane, 1, pl.ds(rows[k], side), :],
                )
                views[k, plane] = pltpu.roll(joined, back_by, 1)

        def view(k, level):
            return views[k, 2 * level], views[k, 2 * level + 1]

        def probe():
            return probe_ref[0], probe_ref[1]

        def add(k, level, patch):
            in_own = lane >= cols[k]
            for part in range(2):
                plane = 2 * level + part
                moved = pltpu.roll(patch[part], cols[k], 1)
                where_now = pl.ds(rows[k], side)
                grad_ref[0, plane, where_now, :] += jnp.where(in_own, moved, 0.0)
                grad_ref[1, plane, where_now, :] += jnp.where(in_own, 0.0, moved)

        members = range(GROUP)
        wave = [times(probe(), view(k, 0)) for k in members]
        for level in range(1, slices):
            moved = two_sided(wave, tables[0], tables[1])
            for k in members:
                kept[k, 2 * level - 2] = moved[k][0]
                kept[k, 2 * level - 1] = moved[k][1]
            wave = [times(view(k, level), moved[k]) for k in members]
        far = two_sided(wave, tables[2], tables[3])
        resid = []
        for k in members:
            real, imag = far[k]
            power = jnp.maximum(real * real + imag * imag, AMPLITUDE_FLOOR * AMPLITUDE_FLOOR)
            measured = amp_ref[meta_ref[64 + first + k]].astype(jnp.float32)
            live = jnp.where(first + k < count, 1.0, 0.0)
            factor = live - (live * measured) * lax.rsqrt(power)
            resid.append((real * factor, imag * factor))
        back = two_sided(resid, tables[3], tables[2])
        for level in range(slices - 1, 0, -1):
            for k in members:
                add(k, level, conj_times((kept[k, 2 * level - 2], kept[k, 2 * level - 1]), back[k]))
            back = two_sided(
                [conj_times(view(k, level), back[k]) for k in members], tables[1], tables[0]
            )
        for k in members:
            add(k, 0, conj_times(probe(), back[k]))
        return carry

    lax.fori_loop(0, (count + GROUP - 1) // GROUP, group_step, 0)


def frame_gradient(meta, own, following, measured, probe_field, planes):
    slices, _, height, side = own.shape
    vmem = pl.BlockSpec(memory_space=pltpu.VMEM)
    return pl.pallas_call(
        frames_kernel,
        out_shape=jax.ShapeDtypeStruct((2, 2 * slices, height, side), jnp.float32),
        in_specs=[pl.BlockSpec(memory_space=pltpu.SMEM)] + [vmem] * 5,
        out_specs=vmem,
        scratch_shapes=[
            pltpu.VMEM((2 * slices, 2, height, side), jnp.float32),
            pltpu.VMEM((4, 2 * side, 2 * side), jnp.bfloat16),
            pltpu.VMEM((GROUP, 2 * slices, side, side), jnp.float32),
            pltpu.VMEM((GROUP, 2 * slices - 2, side, side), jnp.float32),
        ],
        compiler_params=pltpu.CompilerParams(vmem_limit_bytes=48 << 20),
        cost_estimate=pl.CostEstimate(
            flops=16 * 16 * 2**24, bytes_accessed=6 << 20, transcendentals=16 * side * side
        ),
        name="frames",
    )(meta, own, following, measured, probe_field, planes)


def body(amplitudes, positions, probe_field, object_slices):
    frames_held, side, _ = amplitudes.shape
    flat_positions = positions.T.reshape(-1)
    meta = list_frames(flat_positions, frames_held, side, 2)
    planes = jnp.asarray(base_tables(side))
    current = object_slices
    own, following, incoming = opening(flat_positions, amplitudes, current)
    for turn in range(ITERS):
        term = frame_gradient(meta, own, following, incoming, probe_field, planes)
        gathers = turn < ITERS - 1
        current, *panels = exchange(term, current, gathers, 2 + turn)
        if gathers:
            own, following = panels
    return current


def solution(mesh):
    in_specs = (P(("tile", "cuts"), None, None), P(), P(), P("cuts", None, None, "tile"))
    out_specs = P("cuts", None, None, "tile")
    return jax.shard_map(body, mesh=mesh, in_specs=in_specs, out_specs=out_specs, check_vma=False)
```

```python
import functools
import math

import jax
import jax.numpy as jnp
import ml_dtypes
import numpy as np
from jax import lax
from jax.experimental import pallas as pl
from jax.experimental.pallas import tpu as pltpu
from jax.sharding import PartitionSpec as P

ITERS = 2
STEP_SIZE = 0.05
AMPLITUDE_FLOOR = 0.25
GROUP = 8
RING = 4


def base_tables(side):
    index = np.arange(side)
    angle = (index[:, None] * index[None, :] % side) * (2.0 * math.pi / side)
    four = np.exp(-1j * angle) / math.sqrt(side)
    centred = (index + side // 2) % side - side // 2
    chirp = np.exp(-1j * math.pi * centred * centred / (4.0 * side))
    first_row = np.array(
        [np.sum(chirp * np.exp(2j * math.pi * index * shift / side)) for shift in range(side)]
    ) / side
    first_row = 0.5 * (first_row + first_row[(-index) % side])
    prop = first_row[(index[:, None] - index[None, :]) % side]
    planes = np.stack([prop.real, prop.imag, four.real, four.imag])
    return planes.astype(ml_dtypes.bfloat16)


def row_spot(frame):
    return frame // 128 * 256 + frame % 128


def col_spot(frame):
    return row_spot(frame) + 128


def list_kernel(held, shift, capacity, pos_ref, meta_ref):
    tile_count = lax.axis_size("tile")
    cut_count = lax.axis_size("cuts")
    tile = lax.axis_index("tile")
    cut = lax.axis_index("cuts")
    load = 2 * held

    def scan(reader, count):
        begin = col_spot((reader * cut_count + cut) * held)
        for frame in range(held):
            meta_ref[64 + count] = reader * held + frame
            count = count + ((pos_ref[begin + frame] >> shift) == tile).astype(jnp.int32)
        return count

    count = lax.fori_loop(0, tile_count, scan, jnp.int32(0))
    before, slot = jnp.int32(-1), jnp.int32(0)
    for rank in range(load):
        live = rank < count
        packed = jnp.where(live, meta_ref[64 + rank], 0)
        reader = packed // held
        frame = reader * cut_count * held + cut * held + packed % held
        slot = jnp.where(reader == before, slot + 1, 0)
        before = reader
        meta_ref[rank] = jnp.where(live, pos_ref[row_spot(frame)], 0)
        meta_ref[32 + rank] = jnp.where(live, pos_ref[col_spot(frame)] - (tile << shift), 0)
        core, along_z, along_x = reader % 2, reader // 2 % RING, reader // (2 * RING)
        line = jnp.where(core == 0, along_z * RING + along_x, (RING + along_x) * RING + along_z)
        meta_ref[64 + rank] = jnp.where(live, line * capacity + slot, 0)
    meta_ref[96] = count


def list_frames(flat_positions, held, side, capacity):
    return pl.pallas_call(
        functools.partial(list_kernel, held, side.bit_length() - 1, capacity),
        out_shape=jax.ShapeDtypeStruct((128,), jnp.int32),
        in_specs=[pl.BlockSpec(memory_space=pltpu.SMEM)],
        out_specs=pl.BlockSpec(memory_space=pltpu.SMEM),
        name="listing",
    )(flat_positions)


def mesh_copy(source, target, send, recv, tile, cut):
    return pltpu.make_async_remote_copy(
        src_ref=source,
        dst_ref=target,
        send_sem=send,
        recv_sem=recv,
        device_id={"tile": tile, "cuts": cut},
        device_id_type=pl.DeviceIdType.MESH,
    )


def greet(barrier, tile, cut):
    pl.semaphore_signal(
        barrier,
        inc=1,
        device_id={"tile": tile, "cuts": cut},
        device_id_type=pl.DeviceIdType.MESH,
    )


def greet_near(barrier):
    tile_count = lax.axis_size("tile")
    tile = lax.axis_index("tile")
    me = lax.axis_index("cuts")
    has_next = tile < tile_count - 1
    has_prev = tile > 0
    greet(barrier, tile, (me + 1) % RING)
    greet(barrier, tile, (me + 3) % RING)

    @pl.when(has_next)
    def _():
        greet(barrier, tile + 1, me)

    @pl.when(has_prev)
    def _():
        greet(barrier, tile - 1, me)

    return 2 + has_next.astype(jnp.int32) + has_prev.astype(jnp.int32)


class Ring:
    def __init__(self, panel, sends, recvs):
        tile = lax.axis_index("tile")
        me = lax.axis_index("cuts")
        right, left, across = (me + 1) % RING, (me + 3) % RING, (me + 2) % RING

        def copy(index, level, part, cut):
            spot = panel.at[level, part]
            return mesh_copy(spot, spot, sends.at[index], recvs.at[index], tile, cut)

        self.go_right = [copy(part, me, part, right) for part in range(2)]
        self.go_left = [copy(2 + part, me, part, left) for part in range(2)]
        self.from_left = [copy(part, left, part, right) for part in range(2)]
        self.from_right = [copy(2 + part, right, part, left) for part in range(2)]
        self.on_right, self.on_left = copy(4, left, 0, right), copy(5, right, 1, left)
        self.far = [copy(4, across, 0, right), copy(5, across, 1, left)]

    def begin(self, part):
        self.go_right[part].start()
        self.go_left[part].start()

    def take_left(self, part):
        self.from_left[part].wait_recv()
        if part == 0:
            self.on_right.start()

    def take_right(self, part):
        self.from_right[part].wait_recv()
        if part == 1:
            self.on_left.start()

    def take_far(self, part):
        self.far[part].wait_recv()

    def settle(self):
        for copy in self.go_right + self.go_left + [self.on_right, self.on_left]:
            copy.wait_send()


def rim_copies(own_ref, next_ref, sends, recvs):
    tile = lax.axis_index("tile")
    me = lax.axis_index("cuts")
    levels = [me, (me + 3) % RING, (me + 1) % RING, (me + 2) % RING]
    return [
        [
            mesh_copy(
                own_ref.at[level, part],
                next_ref.at[level, part],
                sends.at[2 * role + part],
                recvs.at[2 * role + part],
                tile - 1,
                me,
            )
            for part in range(2)
        ]
        for role, level in enumerate(levels)
    ]


def opening_kernel(
    pos_ref, amp_ref, held_ref, own_ref, next_ref, inbox, mine, below, above, far, outbox,
    amp_box, held_box, fetch, line_send, line_recv, box_send, box_recv,
    rim_send, rim_recv, ring_send, ring_recv, next_send, next_recv,
):
    fetch_held = pltpu.make_async_copy(held_ref, held_box, fetch.at[0])
    fetch_amp = pltpu.make_async_copy(amp_ref, amp_box, fetch.at[1])
    fetch_held.start()
    fetch_amp.start()
    cut_count = lax.axis_size("cuts")
    tile_count = lax.axis_size("tile")
    tile = lax.axis_index("tile")
    me = lax.axis_index("cuts")
    held, side, _ = amp_ref.shape
    shift = side.bit_length() - 1
    core = tile % 2
    along_z = tile // 2 % RING
    along_x = tile // (2 * RING)
    first = (1 - core) * along_x + core * along_z
    second = (1 - core) * along_z + core * along_x

    def tile_at(first_at, second_at, target_core):
        chip = (1 - core) * (first_at * RING + second_at) + core * (second_at * RING + first_at)
        return chip * 2 + target_core

    barrier = pltpu.get_barrier_semaphore()
    expected = greet_near(barrier)
    greet(barrier, tile_at(first, second, 1 - core), me)
    for by in range(1, RING):
        for target_core in range(2):
            greet(barrier, tile_at((first + by) % RING, second, target_core), me)
            greet(barrier, tile_at(first, (second + by) % RING, target_core), me)
            expected = expected + 2
    fetch_held.wait()
    for part in range(2):
        own_ref[me, part] = held_box[0, part].astype(jnp.bfloat16)
    fetch_amp.wait()
    for frame in range(held):
        mine[frame] = amp_box[frame].astype(jnp.bfloat16)
    pl.semaphore_wait(barrier, expected + 1)

    half = held // 2

    def pass_on(index, source, target, begin, count, by):
        return mesh_copy(
            source.at[pl.ds(begin, count)],
            target.at[pl.ds(begin, count)],
            line_send.at[index],
            line_recv.at[index],
            tile_at((first + by) % RING, second, core),
            me,
        )

    before, after, beyond = (first + 3) % RING, (first + 1) % RING, (first + 2) % RING
    go_up, go_down = pass_on(0, mine, below, 0, held, 1), pass_on(1, mine, above, 0, held, 3)
    on_up, on_down = pass_on(2, below, far, 0, half, 1), pass_on(3, above, far, half, half, 3)

    sent = []

    def deal(order, place, line):
        reader = tile_at(place, second, core) * cut_count + me
        owners = [pos_ref[col_spot(reader * held) + frame] >> shift for frame in range(held)]
        for target, (by, swap) in enumerate(
            [(2, 0), (2, 1), (1, 0), (3, 0), (1, 1), (3, 1), (0, 1), (0, 0)]
        ):
            target_core = core if swap == 0 else 1 - core
            goal = tile_at(first, (second + by) % RING, target_core)
            seen = jnp.int32(0)
            pick = [jnp.int32(0), jnp.int32(0)]
            for frame in range(held):
                hit = owners[frame] == goal
                pick[1] = jnp.where(jnp.logical_and(hit, seen == 1), frame, pick[1])
                pick[0] = jnp.where(jnp.logical_and(hit, seen == 0), frame, pick[0])
                seen = seen + hit.astype(jnp.int32)
            for slot in range(2):
                if by == 0 and swap == 0:
                    inbox[core, second, place, slot] = line[pick[slot]]
                else:
                    outbox[order, target, slot] = line[pick[slot]]
            if by or swap:
                copy = mesh_copy(
                    outbox.at[order, target],
                    inbox.at[core, second, place],
                    box_send.at[order, target],
                    box_recv.at[core, second, place],
                    goal,
                    me,
                )
                copy.start()
                sent.append(copy)

    has_next = tile < tile_count - 1
    has_prev = tile > 0
    around = Ring(own_ref, ring_send, ring_recv)
    beside = Ring(next_ref, next_send, next_recv)
    rims = rim_copies(own_ref, next_ref, rim_send, rim_recv)[0]

    @pl.when(has_prev)
    def _():
        for copy in rims:
            copy.start()

    go_up.start()
    go_down.start()
    for part in range(2):
        around.begin(part)
    deal(0, first, mine)

    @pl.when(has_next)
    def _():
        for part in range(2):
            rims[part].wait_recv()
            beside.begin(part)

    for part in range(2):
        around.take_left(part)
        around.take_right(part)
    go_up.wait_recv()
    on_up.start()
    deal(1, before, below)
    go_down.wait_recv()
    on_down.start()
    deal(2, after, above)

    @pl.when(has_next)
    def _():
        for part in range(2):
            beside.take_left(part)
            beside.take_right(part)

    on_up.wait_recv()
    on_down.wait_recv()
    deal(3, beyond, far)
    for part in range(2):
        around.take_far(part)
    around.settle()

    @pl.when(has_next)
    def _():
        for part in range(2):
            beside.take_far(part)
        beside.settle()

    @pl.when(jnp.logical_not(has_next))
    def _():
        next_ref[...] = jnp.zeros_like(next_ref)

    @pl.when(has_prev)
    def _():
        for copy in rims:
            copy.wait_send()

    for sender_core, sender_second in [(core, (second + by) % RING) for by in range(1, RING)] + [
        (1 - core, at) for at in range(RING)
    ]:
        for place in range(RING):
            mesh_copy(
                outbox.at[0, 0],
                inbox.at[sender_core, sender_second, place],
                box_send.at[0, 0],
                box_recv.at[sender_core, sender_second, place],
                tile_at(first, second, 1 - core),
                me,
            ).wait_recv()
    for copy in [go_up, go_down, on_up, on_down] + sent:
        copy.wait_send()


def opening(flat_positions, amplitudes, held):
    frames_held, side, _ = amplitudes.shape
    _, parts, height, width = held.shape
    vmem = pl.BlockSpec(memory_space=pltpu.VMEM)
    panel = jax.ShapeDtypeStruct((RING, parts, height, width), jnp.bfloat16)
    own, following, inbox = pl.pallas_call(
        opening_kernel,
        out_shape=(
            panel,
            panel,
            jax.ShapeDtypeStruct((2, RING, RING, 2, side, side), jnp.bfloat16),
        ),
        in_specs=[pl.BlockSpec(memory_space=pltpu.SMEM)] + [pl.BlockSpec(memory_space=pltpu.HBM)] * 2,
        out_specs=(vmem, vmem, vmem),
        scratch_shapes=[
            *[pltpu.VMEM((frames_held, side, side), jnp.bfloat16)] * 4,
            pltpu.VMEM((RING, 7, 2, side, side), jnp.bfloat16),
            pltpu.VMEM(amplitudes.shape, jnp.float32),
            pltpu.VMEM(held.shape, jnp.float32),
            pltpu.SemaphoreType.DMA((2,)),
            pltpu.SemaphoreType.DMA((4,)),
            pltpu.SemaphoreType.DMA((4,)),
            pltpu.SemaphoreType.DMA((RING, 7)),
            pltpu.SemaphoreType.DMA((2, RING, RING)),
        ]
        + [pltpu.SemaphoreType.DMA((8,))] * 6,
        compiler_params=pltpu.CompilerParams(
            collective_id=1, has_side_effects=True, vmem_limit_bytes=40 << 20
        ),
        name="opening",
    )(flat_positions, amplitudes, held)
    return own, following, inbox.reshape(-1, side, side)


def exchange_kernel(gathers, term_ref, held_ref, new_ref, *refs):
    own_ref, next_ref = refs[:2] if gathers else (None, None)
    refs = refs[2:] if gathers else refs
    out_box, in_box, far_out, far_in, near_out, near_in = refs[:6]
    tile_send, tile_recv, cut_send, cut_recv = refs[6:10]
    tile_count = lax.axis_size("tile")
    tile = lax.axis_index("tile")
    me = lax.axis_index("cuts")
    peers = RING
    right, left, across = (me + 1) % peers, (me + 3) % peers, (me + 2) % peers
    has_next = tile < tile_count - 1
    has_prev = tile > 0
    barrier = pltpu.get_barrier_semaphore()
    expected = greet_near(barrier)

    def to_cut(source, target, sends, recvs, index, cut):
        return mesh_copy(source, target, sends.at[index], recvs.at[index], tile, cut)

    def to_tile(source, target, sends, recvs, index, by):
        return mesh_copy(source, target, sends.at[index], recvs.at[index], tile + by, me)

    def plane(half, level, part):
        return term_ref[half, 2 * level + part]

    order = [across, right, left, me]
    line_up = [(0, 0), (0, 1), (1, 1), (2, 0), (1, 0), (2, 1), (3, 0), (3, 1)]
    forward = {
        (k, part): to_tile(
            out_box.at[k, part], in_box.at[k, part], tile_send, tile_recv, 2 * k + part, 1
        )
        for k, part in line_up
    }

    @pl.when(has_next)
    def _():
        for k, part in line_up:
            out_box[k, part] = plane(1, order[k], part).astype(jnp.bfloat16)

    @pl.when(jnp.logical_not(has_prev))
    def _():
        in_box[...] = jnp.zeros_like(in_box)

    pl.semaphore_wait(barrier, expected)

    @pl.when(has_next)
    def _():
        for pair in line_up:
            forward[pair].start()

    def joined(k, part):
        @pl.when(has_prev)
        def _():
            forward[k, part].wait_recv()

        return plane(0, order[k], part) + in_box[k, part].astype(jnp.float32)

    far_right = to_cut(far_out.at[0], far_in.at[0], cut_send, cut_recv, 0, right)
    far_left = to_cut(far_out.at[1], far_in.at[1], cut_send, cut_recv, 1, left)
    near_right = [
        to_cut(near_out.at[0, part], near_in.at[0, part], cut_send, cut_recv, 2 + part, right)
        for part in range(2)
    ]
    near_left = [
        to_cut(near_out.at[1, part], near_in.at[1, part], cut_send, cut_recv, 4 + part, left)
        for part in range(2)
    ]
    far_out[0] = joined(0, 0).astype(jnp.bfloat16)
    far_right.start()
    far_out[1] = joined(0, 1).astype(jnp.bfloat16)
    far_left.start()
    near_out[0, 1] = joined(1, 1).astype(jnp.bfloat16)
    near_right[1].start()
    near_out[1, 0] = joined(2, 0).astype(jnp.bfloat16)
    near_left[0].start()
    near_own = joined(1, 0)
    far_right.wait_recv()
    near_out[0, 0] = (near_own + far_in[0].astype(jnp.float32)).astype(jnp.bfloat16)
    near_right[0].start()
    near_own = joined(2, 1)
    far_left.wait_recv()
    near_out[1, 1] = (near_own + far_in[1].astype(jnp.float32)).astype(jnp.bfloat16)
    near_left[1].start()
    for part in range(2):
        new_ref[0, part] = joined(3, part)
    if gathers:
        around = Ring(own_ref, *refs[12:14])
        rims = rim_copies(own_ref, next_ref, *refs[10:12])
    for part in range(2):
        near_right[part].wait_recv()
        near_left[part].wait_recv()
        share = (
            new_ref[0, part]
            + near_in[0, part].astype(jnp.float32)
            + near_in[1, part].astype(jnp.float32)
        )
        fresh = held_ref[0, part] - STEP_SIZE * share
        new_ref[0, part] = fresh
        if gathers:
            own_ref[me, part] = fresh.astype(jnp.bfloat16)
            around.begin(part)

            @pl.when(has_prev)
            def _():
                rims[0][part].start()

    if gathers:

        def pass_rim(role, part):
            @pl.when(has_prev)
            def _():
                rims[role][part].start()

        for part in range(2):
            around.take_left(part)
            pass_rim(1, part)
            around.take_right(part)
            pass_rim(2, part)
        for part in range(2):
            around.take_far(part)
            pass_rim(3, part)

        @pl.when(has_next)
        def _():
            for pair in rims:
                for copy in pair:
                    copy.wait_recv()

        @pl.when(jnp.logical_not(has_next))
        def _():
            next_ref[...] = jnp.zeros_like(next_ref)

        around.settle()

        @pl.when(has_prev)
        def _():
            for pair in rims:
                for copy in pair:
                    copy.wait_send()

    for copy in [far_right, far_left] + near_right + near_left:
        copy.wait_send()

    @pl.when(has_next)
    def _():
        for pair in line_up:
            forward[pair].wait_send()


def exchange(term, held, gathers, number):
    _, parts, height, width = held.shape
    vmem = pl.BlockSpec(memory_space=pltpu.VMEM)
    outs = [jax.ShapeDtypeStruct(held.shape, jnp.float32)]
    scratch = [
        pltpu.VMEM((RING, parts, height, width), jnp.bfloat16),
        pltpu.VMEM((RING, parts, height, width), jnp.bfloat16),
        pltpu.VMEM((2, height, width), jnp.bfloat16),
        pltpu.VMEM((2, height, width), jnp.bfloat16),
        pltpu.VMEM((2, parts, height, width), jnp.bfloat16),
        pltpu.VMEM((2, parts, height, width), jnp.bfloat16),
    ] + [pltpu.SemaphoreType.DMA((8,))] * 4
    if gathers:
        outs += [jax.ShapeDtypeStruct((RING, parts, height, width), jnp.bfloat16)] * 2
        scratch += [pltpu.SemaphoreType.DMA((8,))] * 4
    return pl.pallas_call(
        functools.partial(exchange_kernel, gathers),
        out_shape=tuple(outs),
        in_specs=[vmem] * 2,
        out_specs=tuple([vmem] * len(outs)),
        scratch_shapes=scratch,
        compiler_params=pltpu.CompilerParams(
            collective_id=number, has_side_effects=True, vmem_limit_bytes=40 << 20
        ),
        name="exchange",
    )(term, held)


def times(left, right):
    return left[0] * right[0] - left[1] * right[1], left[0] * right[1] + left[1] * right[0]


def conj_times(left, right):
    return left[0] * right[0] + left[1] * right[1], left[0] * right[1] - left[1] * right[0]


def two_sided(fields, right_table, left_table):
    side = fields[0][0].shape[-1]
    results = []
    for pair in range(0, len(fields), 2):
        rows = [
            jnp.concatenate([part.astype(jnp.bfloat16) for part in field], axis=1)
            for field in fields[pair : pair + 2]
        ]
        first = jnp.dot(
            jnp.concatenate(rows, axis=0), right_table, preferred_element_type=jnp.float32
        ).astype(jnp.bfloat16)
        turned = jnp.concatenate(
            [
                jnp.concatenate([first[:side, :side], first[side:, :side]], axis=1),
                jnp.concatenate([first[:side, side:], first[side:, side:]], axis=1),
            ],
            axis=0,
        )
        second = jnp.dot(left_table, turned, preferred_element_type=jnp.float32)
        results.append((second[:side, :side], second[side:, :side]))
        results.append((second[:side, side:], second[side:, side:]))
    return results


def frames_kernel(
    meta_ref, own_ref, next_ref, amp_ref, probe_hbm, planes_hbm, grad_ref,
    panel, tables, views, kept, probe_ref, planes_ref, fetch,
):
    fetch_probe = pltpu.make_async_copy(probe_hbm, probe_ref, fetch.at[0])
    fetch_planes = pltpu.make_async_copy(planes_hbm, planes_ref, fetch.at[1])
    fetch_probe.start()
    fetch_planes.start()
    slices = own_ref.shape[0]
    side = own_ref.shape[-1]
    for level in range(slices):
        for part in range(2):
            plane = 2 * level + part
            panel[plane, 0] = own_ref[level, part].astype(jnp.float32)
            panel[plane, 1] = next_ref[level, part].astype(jnp.float32)
    grad_ref[...] = jnp.zeros_like(grad_ref)
    fetch_probe.wait()
    fetch_planes.wait()
    for kind in range(2):
        real, imag = planes_ref[2 * kind], planes_ref[2 * kind + 1]
        tables[2 * kind, :side, :side] = real
        tables[2 * kind, side:, side:] = real
        tables[2 * kind, :side, side:] = imag
        tables[2 * kind, side:, :side] = -imag
        tables[2 * kind + 1, :side, :side] = real
        tables[2 * kind + 1, side:, side:] = real
        tables[2 * kind + 1, :side, side:] = -imag
        tables[2 * kind + 1, side:, :side] = imag
    lane = lax.broadcasted_iota(jnp.int32, (side, side), 1)
    count = meta_ref[96]

    def group_step(group, carry):
        first = group * GROUP
        rows = [meta_ref[first + k] for k in range(GROUP)]
        cols = [meta_ref[32 + first + k] for k in range(GROUP)]
        for k in range(GROUP):
            from_own = lane >= cols[k]
            back_by = (side - cols[k]) % side
            for plane in range(2 * slices):
                joined = jnp.where(
                    from_own,
                    panel[plane, 0, pl.ds(rows[k], side), :],
                    panel[plane, 1, pl.ds(rows[k], side), :],
                )
                views[k, plane] = pltpu.roll(joined, back_by, 1)

        def view(k, level):
            return views[k, 2 * level], views[k, 2 * level + 1]

        def probe():
            return probe_ref[0], probe_ref[1]

        def add(k, level, patch):
            in_own = lane >= cols[k]
            for part in range(2):
                plane = 2 * level + part
                moved = pltpu.roll(patch[part], cols[k], 1)
                where_now = pl.ds(rows[k], side)
                grad_ref[0, plane, where_now, :] += jnp.where(in_own, moved, 0.0)
                grad_ref[1, plane, where_now, :] += jnp.where(in_own, 0.0, moved)

        members = range(GROUP)
        wave = [times(probe(), view(k, 0)) for k in members]
        for level in range(1, slices):
            moved = two_sided(wave, tables[0], tables[1])
            for k in members:
                kept[k, 2 * level - 2] = moved[k][0]
                kept[k, 2 * level - 1] = moved[k][1]
            wave = [times(view(k, level), moved[k]) for k in members]
        far = two_sided(wave, tables[2], tables[3])
        resid = []
        for k in members:
            real, imag = far[k]
            power = jnp.maximum(real * real + imag * imag, AMPLITUDE_FLOOR * AMPLITUDE_FLOOR)
            measured = amp_ref[meta_ref[64 + first + k]].astype(jnp.float32)
            live = jnp.where(first + k < count, 1.0, 0.0)
            factor = live - (live * measured) * lax.rsqrt(power)
            resid.append((real * factor, imag * factor))
        back = two_sided(resid, tables[3], tables[2])
        for level in range(slices - 1, 0, -1):
            for k in members:
                add(k, level, conj_times((kept[k, 2 * level - 2], kept[k, 2 * level - 1]), back[k]))
            back = two_sided(
                [conj_times(view(k, level), back[k]) for k in members], tables[1], tables[0]
            )
        for k in members:
            add(k, 0, conj_times(probe(), back[k]))
        return carry

    lax.fori_loop(0, (count + GROUP - 1) // GROUP, group_step, 0)


def frame_gradient(meta, own, following, measured, probe_field, planes):
    slices, _, height, side = own.shape
    vmem = pl.BlockSpec(memory_space=pltpu.VMEM)
    return pl.pallas_call(
        frames_kernel,
        out_shape=jax.ShapeDtypeStruct((2, 2 * slices, height, side), jnp.float32),
        in_specs=[pl.BlockSpec(memory_space=pltpu.SMEM)]
        + [vmem] * 3
        + [pl.BlockSpec(memory_space=pltpu.HBM)] * 2,
        out_specs=vmem,
        scratch_shapes=[
            pltpu.VMEM((2 * slices, 2, height, side), jnp.float32),
            pltpu.VMEM((4, 2 * side, 2 * side), jnp.bfloat16),
            pltpu.VMEM((GROUP, 2 * slices, side, side), jnp.float32),
            pltpu.VMEM((GROUP, 2 * slices - 2, side, side), jnp.float32),
            pltpu.VMEM(probe_field.shape, jnp.float32),
            pltpu.VMEM(planes.shape, jnp.bfloat16),
            pltpu.SemaphoreType.DMA((2,)),
        ],
        compiler_params=pltpu.CompilerParams(vmem_limit_bytes=48 << 20),
        cost_estimate=pl.CostEstimate(
            flops=16 * 16 * 2**24, bytes_accessed=6 << 20, transcendentals=16 * side * side
        ),
        name="frames",
    )(meta, own, following, measured, probe_field, planes)


def body(amplitudes, positions, probe_field, object_slices):
    frames_held, side, _ = amplitudes.shape
    flat_positions = positions.reshape(-1, 128, 2).transpose(0, 2, 1).reshape(-1)
    meta = list_frames(flat_positions, frames_held, side, 2)
    planes = jnp.asarray(base_tables(side))
    current = object_slices
    own, following, incoming = opening(flat_positions, amplitudes, current)
    for turn in range(ITERS):
        term = frame_gradient(meta, own, following, incoming, probe_field, planes)
        gathers = turn < ITERS - 1
        current, *panels = exchange(term, current, gathers, 2 + turn)
        if gathers:
            own, following = panels
    return current


def solution(mesh):
    in_specs = (P(("tile", "cuts"), None, None), P(), P(), P("cuts", None, None, "tile"))
    out_specs = P("cuts", None, None, "tile")
    return jax.shard_map(body, mesh=mesh, in_specs=in_specs, out_specs=out_specs, check_vma=False)
```
